1024 devices in a mesh: dp: 8 (over z_hi, core), fsdp: 128 (over x, z_lo, y).
Axes of the slice: x: 4, y: 4, z: 32 (z_hi: 4, z_lo: 8; z = z_hi * 8 + z_lo), core: 2. Of those that a mesh axis runs over, the one named last changes fastest.
Arguments:
- attention_input: bfloat16 [8192, 1536], P('fsdp', 'dp')
- feedforward_input: bfloat16 [14336, 1536], P('fsdp', 'dp')
- attention_cotangent: bfloat16 [8192, 1536], P(('dp', 'fsdp'))
- feedforward_cotangent: bfloat16 [8192, 1536], P(('dp', 'fsdp'))
- lengths: int32 [24], replicated, may hold values from 16 to 64, as said below
- groups: int32 [24], replicated, may hold values from 0 to 3, as said below
- attention_weight: bfloat16 [8192, 8192], P('fsdp', 'dp'), may hold values from -0.29882812 to 0.29882812
- attention_moment: bfloat16 [8192, 8192], P('fsdp', 'dp'), may hold values from -0.59765625 to 0.59765625
- attention_second: bfloat16 [8192, 8192], P('fsdp', 'dp'), may hold values from 0.0099487305 to 1
- feedforward_weight: bfloat16 [14336, 8192], P('fsdp', 'dp'), may hold values from -0.29882812 to 0.29882812
- feedforward_moment: bfloat16 [14336, 8192], P('fsdp', 'dp'), may hold values from -0.59765625 to 0.59765625
- feedforward_second: bfloat16 [14336, 8192], P('fsdp', 'dp'), may hold values from 0.0099487305 to 1
Outputs:
- new_attention_weight: bfloat16 [8192, 8192], P('fsdp', 'dp')
- new_attention_moment: bfloat16 [8192, 8192], P('fsdp', 'dp')
- new_attention_second: bfloat16 [8192, 8192], P('fsdp', 'dp')
- new_feedforward_weight: bfloat16 [14336, 8192], P('fsdp', 'dp')
- new_feedforward_moment: bfloat16 [14336, 8192], P('fsdp', 'dp')
- new_feedforward_second: bfloat16 [14336, 8192], P('fsdp', 'dp')
The draws below stay inside these ranges and needn't reach their ends.
Inputs may be any that keep to these rules, and one draw needn't show every extreme that they name: `lengths`: some example has exactly 64 live tokens. `groups`: every group has at least one example.
All inputs are finite; a program needn't handle non-finite values.
Results may differ from the reference program's by a relative error of at most 0.0038.
Values may be sent and summed in bfloat16 or wider, within the bound.
No kernel may reach another device: no remote copies, remote signals or barrier semaphores. Data moves between devices by JAX's collectives and lax.ppermute only.
A program may use at most 64 MiB of HBM per device.

```python
import math
import jax
import jax.numpy as jnp
from jax import lax

D = 8192
FF_WIN = 14336
SLOT = 64
GROUPS = 4
EXAMPLES = 24
TOKENS = 1536


region_count = 8


def scaled_field(key, height, magnitude):
    jitter_key, row_key, region_key = jax.random.split(key, 3)
    jitter = jax.random.normal(jitter_key, (height, TOKENS), jnp.float32)
    row_factor = jnp.exp(jax.random.uniform(row_key, (height, EXAMPLES, 1), jnp.float32, math.log(0.5), math.log(2.0)))
    region_factor = jnp.exp(jax.random.uniform(region_key, (region_count, EXAMPLES, 1), jnp.float32, math.log(0.2), math.log(5.0)))
    region_of_row = jnp.arange(height, dtype=jnp.int32) * region_count // height
    region_rows = region_factor[region_of_row]
    spread = jnp.broadcast_to(row_factor * region_rows, (height, EXAMPLES, SLOT)).reshape(height, TOKENS)
    return magnitude * jitter * spread


def draw_attention_input(key, part):
    return scaled_field(jax.random.fold_in(key, 11), D, 1.0).astype(jnp.bfloat16)


def draw_feedforward_input(key, part):
    return scaled_field(jax.random.fold_in(key, 12), FF_WIN, 1.0).astype(jnp.bfloat16)


def draw_attention_cotangent(key, part):
    return scaled_field(jax.random.fold_in(key, 13), D, 0.05).astype(jnp.bfloat16)


def draw_feedforward_cotangent(key, part):
    return scaled_field(jax.random.fold_in(key, 14), D, 0.05).astype(jnp.bfloat16)


def draw_lengths(key, part):
    values_key, marked_key = jax.random.split(jax.random.fold_in(key, 21))
    values = jax.random.randint(values_key, (EXAMPLES,), max(SLOT // 4, 1), SLOT + 1)
    marked = jax.random.randint(marked_key, (), 0, EXAMPLES)
    return jnp.where(jnp.arange(EXAMPLES) == marked, SLOT, values).astype(jnp.int32)


def draw_groups(key, part):
    values_key, shuffle_key = jax.random.split(jax.random.fold_in(key, 22))
    values = jax.random.randint(values_key, (EXAMPLES,), 0, GROUPS)
    shuffled = jax.random.permutation(shuffle_key, EXAMPLES)
    return values.at[shuffled[:GROUPS]].set(jnp.arange(GROUPS, dtype=jnp.int32)).astype(jnp.int32)


def level_of(key, extent, pieces, smallest, largest):
    level = 1.0
    for dim, blocks in pieces:
        heights = jax.random.uniform(jax.random.fold_in(jax.random.fold_in(key, 6), dim), (blocks,), jnp.float32, smallest / len(pieces), largest / len(pieces))
        level = level * jnp.repeat(jnp.exp(heights), extent[dim] // blocks).reshape((-1,) + (1,) * (len(extent) - 1 - dim))
    return level


def scatter_about(stream_key, extent, deviation, reach, shards=(), kind=jnp.bfloat16):
    entries = jax.random.normal(stream_key, extent, jnp.float32) * deviation
    if len(shards) > 0:
        entries = level_of(stream_key, extent, shards, -0.22, 0.18) * entries
    return jnp.clip(entries, min=-reach, max=reach).astype(kind)


def setup_inputs(seed: int = 0) -> dict:
    seeds = jax.random.split(jax.random.key(seed), 13)
    return {
        "attention_input": draw_attention_input(jax.random.fold_in(seeds[12], 71), 0),
        "feedforward_input": draw_feedforward_input(jax.random.fold_in(seeds[12], 71), 0),
        "attention_cotangent": draw_attention_cotangent(jax.random.fold_in(seeds[12], 71), 0),
        "feedforward_cotangent": draw_feedforward_cotangent(jax.random.fold_in(seeds[12], 71), 0),
        "lengths": draw_lengths(jax.random.fold_in(seeds[12], 71), 0),
        "groups": draw_groups(jax.random.fold_in(seeds[12], 71), 0),
        "attention_weight": scatter_about(seeds[6], (D, D), 0.05, 0.29882812, ((0, 128), (1, 8))),
        "attention_moment": scatter_about(seeds[7], (D, D), 0.1, 0.59765625, ((0, 128), (1, 8))),
        "attention_second": jnp.clip(jnp.exp(math.log(1.0) - 4.61031033 * jax.random.uniform(seeds[8], (D, D), jnp.float32) ** level_of(seeds[8], (D, D), ((0, 128), (1, 8)), -0.2, 0.2)), 0.0099487305, 1.0).astype(jnp.bfloat16),
        "feedforward_weight": scatter_about(seeds[9], (FF_WIN, D), 0.05, 0.29882812, ((0, 128), (1, 8))),
        "feedforward_moment": scatter_about(seeds[10], (FF_WIN, D), 0.1, 0.59765625, ((0, 128), (1, 8))),
        "feedforward_second": jnp.clip(jnp.exp(math.log(1.0) - 4.61031033 * jax.random.uniform(seeds[11], (FF_WIN, D), jnp.float32) ** level_of(seeds[11], (FF_WIN, D), ((0, 128), (1, 8)), -0.2, 0.2)), 0.0099487305, 1.0).astype(jnp.bfloat16),
    }


first_decay = 0.9
second_decay = 0.95
first_bias = 1.0 - 0.9 ** 10
second_bias = 1.0 - 0.95 ** 10
learn_rate = 0.01
weight_decay = 0.1
epsilon = 1e-08
norm_epsilon = 1e-06

def live_tokens(lengths, slot_len):
    position = lax.broadcasted_iota(jnp.int32, (lengths.shape[0], slot_len), 1)
    return (position < lengths[:, None]).reshape(-1)

def example_norms(inputs, cotangents, second, slot_len):
    precond = 1.0 / (jnp.sqrt(second.astype(jnp.float32)) + epsilon)
    inputs_wide = inputs.astype(jnp.float32)
    cotangents_wide = cotangents.astype(jnp.float32)
    example_count = inputs.shape[1] // slot_len

    def one_example(example, norm_vals):
        inputs_slot = lax.dynamic_slice_in_dim(inputs_wide, example * slot_len, slot_len, 1)
        grads_slot = lax.dynamic_slice_in_dim(cotangents_wide, example * slot_len, slot_len, 1)
        tile_block = lax.dot_general(inputs_slot, grads_slot, (((1,), (1,)), ((), ())), preferred_element_type=jnp.float32)
        return norm_vals.at[example].set(jnp.sum(tile_block * tile_block * precond))
    return lax.fori_loop(0, example_count, one_example, jnp.zeros((example_count,), jnp.float32))

def importance(norm_vals, groups):
    strength = jnp.sqrt(norm_vals + norm_epsilon)
    same_group = (groups[:, None] == groups[None, :]).astype(jnp.float32)
    group_total = lax.optimization_barrier(jnp.sum(same_group * strength[None, :], axis=1))
    group_count = lax.optimization_barrier(jnp.sum(same_group, axis=1))
    return group_count * strength / group_total

def weighted_gradient(inputs, cotangents, token_weight, example_count):
    scaled = (inputs.astype(jnp.float32) * token_weight[None, :]).astype(jnp.bfloat16)
    product = lax.dot_general(scaled.astype(jnp.float32), cotangents.astype(jnp.float32), (((1,), (1,)), ((), ())), preferred_element_type=jnp.float32)
    return product / example_count

def adamw_step(weight, moment, second, gradient):
    moment_new = first_decay * moment.astype(jnp.float32) + (1.0 - first_decay) * gradient
    second_new = second_decay * second.astype(jnp.float32) + (1.0 - second_decay) * gradient * gradient
    step_dir = moment_new / first_bias / (jnp.sqrt(second_new / second_bias) + epsilon)
    weight_wide = weight.astype(jnp.float32)
    updated = weight_wide - learn_rate * (step_dir + weight_decay * weight_wide)
    return (updated.astype(jnp.bfloat16), moment_new.astype(jnp.bfloat16), second_new.astype(jnp.bfloat16))

def reference(attention_input, feedforward_input, attention_cotangent, feedforward_cotangent, lengths, groups, attention_weight, attention_moment, attention_second, feedforward_weight, feedforward_moment, feedforward_second):
    example_count = lengths.shape[0]
    slot_len = attention_input.shape[1] // example_count
    live_mask = live_tokens(lengths, slot_len)
    attention_live = jnp.where(live_mask[None, :], attention_input, jnp.zeros_like(attention_input))
    feedforward_live = jnp.where(live_mask[None, :], feedforward_input, jnp.zeros_like(feedforward_input))
    norm_vals = example_norms(attention_live, attention_cotangent, attention_second, slot_len) + example_norms(feedforward_live, feedforward_cotangent, feedforward_second, slot_len)
    weights = importance(norm_vals, groups)
    token_weight = jnp.repeat(weights, slot_len) * live_mask.astype(jnp.float32)
    attention_grad = weighted_gradient(attention_live, attention_cotangent, token_weight, example_count)
    feedforward_grad = weighted_gradient(feedforward_live, feedforward_cotangent, token_weight, example_count)
    attention_new = adamw_step(attention_weight, attention_moment, attention_second, attention_grad)
    feedforward_new = adamw_step(feedforward_weight, feedforward_moment, feedforward_second, feedforward_grad)
    return (attention_new[0], attention_new[1], attention_new[2], feedforward_new[0], feedforward_new[1], feedforward_new[2])
```

```python
import functools

import jax
import jax.numpy as jnp
from jax import lax
from jax.experimental import pallas as pl
from jax.experimental.pallas import tpu as pltpu
from jax.sharding import Mesh
from jax.sharding import PartitionSpec as P

DP = ("dp_0", "dp_1")
FSDP = ("fsdp_0", "fsdp_1", "fsdp_2")
DP_FSDP = ("dp_0", "dp_1", "fsdp_0", "fsdp_1", "fsdp_2")


first_decay = 0.9
second_decay = 0.95
first_bias = 1.0 - 0.9**10
second_bias = 1.0 - 0.95**10
learn_rate = 0.01
weight_decay = 0.1
epsilon = 1e-08
norm_epsilon = 1e-06


def token_rows(arrays):
    both = jnp.concatenate(arrays, axis=0)
    filled = lax.all_gather(both, DP, axis=1, tiled=True)
    return filled


def column_rows(arrays):
    both = jnp.concatenate(arrays, axis=1)
    run = lax.all_gather(both, "fsdp_1", axis=0, tiled=False)
    plane = lax.all_gather(run, ("fsdp_0", "fsdp_2"), axis=0, tiled=False)
    plane = plane.reshape(4, 4, *run.shape)
    ordered = plane.transpose(0, 2, 1, 3, 4)
    return ordered.reshape(-1, both.shape[1])


def sum_everywhere(row):
    peers = lax.axis_size(FSDP)
    spread = jnp.broadcast_to(row[None, :], (peers, row.shape[0]))
    met = lax.all_to_all(spread, FSDP, 0, 0, tiled=True)
    part = jnp.sum(met, axis=0, keepdims=True)
    return jnp.sum(lax.all_gather(part, DP, axis=0, tiled=True), axis=0)


def live_tokens(lengths, slot_len):
    position = lax.broadcasted_iota(jnp.int32, (lengths.shape[0], slot_len), 1)
    return (position < lengths[:, None]).reshape(-1)


def norm_kernel(slot, lengths_ref, x_ref, ca_ref, cf_ref, va_ref, vf_ref, out_ref, pa_ref, pf_ref):
    step = pl.program_id(0)

    @pl.when(step == 0)
    def _():
        pa_ref[...] = 1.0 / (jnp.sqrt(va_ref[...].astype(jnp.float32)) + epsilon)
        pf_ref[...] = 1.0 / (jnp.sqrt(vf_ref[...].astype(jnp.float32)) + epsilon)
        out_ref[...] = jnp.zeros_like(out_ref)

    x = x_ref[...]
    rows_a, width = pa_ref.shape
    rows = x.shape[0]
    block = x.shape[1]
    per = block // slot
    position = lax.broadcasted_iota(jnp.int32, (rows, block), 1)
    chosen = []
    for j in range(per):
        live = lengths_ref[step * per + j]
        chosen.append(
            jnp.where((position >= j * slot) & (position < j * slot + live), x, jnp.zeros_like(x))
        )
    wide = 256
    for j in range(per):
        part = jnp.zeros((8, wide), jnp.float32)
        for at in range(0, width, wide):
            for c_ref, p_ref, low, high in (
                (ca_ref, pa_ref, 0, rows_a),
                (cf_ref, pf_ref, rows_a, rows),
            ):
                tile = lax.dot_general(
                    chosen[j][low:high],
                    c_ref[at : at + wide, :],
                    (((1,), (1,)), ((), ())),
                    preferred_element_type=jnp.float32,
                )
                share = tile * tile * p_ref[:, at : at + wide]
                part = part + jnp.sum(share.reshape(-1, 8, wide), axis=0)
        total = jnp.sum(part)
        row = lax.broadcasted_iota(jnp.int32, out_ref.shape, 1)
        out_ref[...] = out_ref[...] + jnp.where(row == step * per + j, total, 0.0)

def norms(x, columns, va, vf, lengths, slot, block=256):
    rows, tokens = x.shape
    width = columns.shape[0]
    steps = tokens // block
    return pl.pallas_call(
        functools.partial(norm_kernel, slot),
        out_shape=jax.ShapeDtypeStruct((8, 128), jnp.float32),
        grid=(steps,),
        in_specs=[
            pl.BlockSpec(memory_space=pltpu.SMEM),
            pl.BlockSpec((rows, block), lambda i: (0, i)),
            pl.BlockSpec((width, block), lambda i: (0, i)),
            pl.BlockSpec((width, block), lambda i, n=steps: (0, i + n)),
            pl.BlockSpec(va.shape, lambda i: (0, 0)),
            pl.BlockSpec(vf.shape, lambda i: (0, 0)),
        ],
        out_specs=pl.BlockSpec((8, 128), lambda i: (0, 0)),
        scratch_shapes=[pltpu.VMEM(va.shape, jnp.float32), pltpu.VMEM(vf.shape, jnp.float32)],
        compiler_params=pltpu.CompilerParams(dimension_semantics=("arbitrary",)),
        name="norms",
    )(lengths, x, columns, columns, va, vf)


def importance(norm_vals, groups):
    strength = jnp.sqrt(norm_vals + norm_epsilon)
    same_group = (groups[:, None] == groups[None, :]).astype(jnp.float32)
    group_total = jnp.sum(same_group * strength[None, :], axis=1)
    group_count = jnp.sum(same_group, axis=1)
    return group_count * strength / group_total


def weighted_gradient(inputs, cotangents, token_weight, example_count):
    scaled = (inputs.astype(jnp.float32) * token_weight[None, :]).astype(jnp.bfloat16)
    product = lax.dot_general(
        scaled, cotangents, (((1,), (1,)), ((), ())), preferred_element_type=jnp.float32
    )
    return product / example_count


def adamw_step(weight, moment, second, gradient):
    moment_new = first_decay * moment.astype(jnp.float32) + (1.0 - first_decay) * gradient
    second_new = (
        second_decay * second.astype(jnp.float32) + (1.0 - second_decay) * gradient * gradient
    )
    step_dir = moment_new / first_bias / (jnp.sqrt(second_new / second_bias) + epsilon)
    weight_wide = weight.astype(jnp.float32)
    updated = weight_wide - learn_rate * (step_dir + weight_decay * weight_wide)
    return (
        updated.astype(jnp.bfloat16),
        moment_new.astype(jnp.bfloat16),
        second_new.astype(jnp.bfloat16),
    )


def per_device(
    attention_input,
    feedforward_input,
    attention_cotangent,
    feedforward_cotangent,
    lengths,
    groups,
    attention_weight,
    attention_moment,
    attention_second,
    feedforward_weight,
    feedforward_moment,
    feedforward_second,
):
    example_count = lengths.shape[0]
    columns = column_rows((attention_cotangent, feedforward_cotangent))
    inputs = token_rows((attention_input, feedforward_input))
    tokens = inputs.shape[1]
    slot_len = tokens // example_count
    live_mask = live_tokens(lengths, slot_len)
    row = norms(inputs, columns, attention_second, feedforward_second, lengths, slot_len)
    norm_vals = sum_everywhere(row[0])[:example_count]
    weights = importance(norm_vals, groups)
    token_weight = jnp.repeat(weights, slot_len) * live_mask.astype(jnp.float32)
    attention_rows = attention_input.shape[0]
    live = jnp.where(live_mask[None, :], inputs, jnp.zeros_like(inputs))
    attention_grad = weighted_gradient(
        live[:attention_rows], columns[:, :tokens], token_weight, example_count
    )
    feedforward_grad = weighted_gradient(
        live[attention_rows:], columns[:, tokens:], token_weight, example_count
    )
    attention_new = adamw_step(attention_weight, attention_moment, attention_second, attention_grad)
    feedforward_new = adamw_step(
        feedforward_weight, feedforward_moment, feedforward_second, feedforward_grad
    )
    return (
        attention_new[0],
        attention_new[1],
        attention_new[2],
        feedforward_new[0],
        feedforward_new[1],
        feedforward_new[2],
    )


def solution(mesh):
    finer = Mesh(
        mesh.devices.reshape(4, 2, 4, 8, 4), ("dp_0", "dp_1", "fsdp_0", "fsdp_1", "fsdp_2")
    )
    in_specs = (
        P(FSDP, DP),
        P(FSDP, DP),
        P(DP_FSDP, None),
        P(DP_FSDP, None),
        P(),
        P(),
        P(FSDP, DP),
        P(FSDP, DP),
        P(FSDP, DP),
        P(FSDP, DP),
        P(FSDP, DP),
        P(FSDP, DP),
    )
    out_specs = (P(FSDP, DP), P(FSDP, DP), P(FSDP, DP), P(FSDP, DP), P(FSDP, DP), P(FSDP, DP))
    return jax.shard_map(
        per_device, mesh=finer, in_specs=in_specs, out_specs=out_specs, check_vma=False
    )
```

```python
import functools

import jax
import jax.numpy as jnp
from jax import lax
from jax.experimental import pallas as pl
from jax.experimental.pallas import tpu as pltpu
from jax.sharding import Mesh
from jax.sharding import PartitionSpec as P

DP = ("dp_0", "dp_1")
FSDP = ("fsdp_0", "fsdp_1", "fsdp_2")
DP_FSDP = ("dp_0", "dp_1", "fsdp_0", "fsdp_1", "fsdp_2")


first_decay = 0.9
second_decay = 0.95
first_bias = 1.0 - 0.9**10
second_bias = 1.0 - 0.95**10
learn_rate = 0.01
weight_decay = 0.1
epsilon = 1e-08
norm_epsilon = 1e-06


LEAP = (0, -1, 1, 2)


def turn(value, axis, by):
    size = lax.axis_size(axis)
    return lax.ppermute(value, axis, [(i, (i + by) % size) for i in range(size)])


def ring_pieces(value, axis):
    return [value] + [turn(value, axis, -leap) for leap in LEAP[1:]]


def z_run(arrays):
    both = jnp.concatenate(arrays, axis=1)
    peers = lax.axis_size("fsdp_1")
    spread = jnp.broadcast_to(both[None], (peers,) + both.shape)
    return lax.all_to_all(spread, "fsdp_1", 0, 0, tiled=False)


def packed_inputs(arrays):
    both = jnp.concatenate(arrays, axis=0)
    rows, width = both.shape
    lanes = 128
    rest = both[:, lanes:]
    parts = lanes // (width - lanes)
    tail = jnp.concatenate(jnp.split(rest, parts, axis=0), axis=1)
    return jnp.concatenate([both[:, :lanes], tail], axis=0)


def unpacked_inputs(blocks, rows, width):
    count, _, lanes = blocks.shape
    body = blocks[:, :rows]
    rest = width - lanes
    tail = jnp.concatenate([blocks[:, rows:, at : at + rest] for at in range(0, lanes, rest)], axis=1)
    whole = jnp.concatenate([body, tail], axis=2)
    return whole.transpose(1, 0, 2).reshape(rows, count * width)


def sum_shares(spread):
    met = lax.all_to_all(spread, FSDP, 0, 0, tiled=True)
    part = jnp.sum(met, axis=0, keepdims=True)
    return lax.all_gather(part, DP, axis=0, tiled=True)


def column_copies(r, spot_ref, pieces, ca_ref, cf_ref, sems):
    a0, a1, a2, a3, a4, f0, f1, f2, f3, f4 = pieces
    ring = ca_ref.shape[2]
    half = ring // 2
    at_y = [lax.rem(spot_ref[1] + (leap + ring), ring) for leap in LEAP]
    last = a3.at[r] if r < half else a4.at[r - half]
    sources = [(a0.at[r], ca_ref, 0), (a1.at[r], ca_ref, 1), (a2.at[r], ca_ref, 2), (last, ca_ref, 3)]
    for y in range(ring):
        if r < 3:
            source = (f0, f1, f2)[r].at[y]
        else:
            source = f3.at[y] if y < half else f4.at[y - half]
        sources.append((source, cf_ref, y))
    return [
        pltpu.make_async_copy(source, to.at[r, :, at_y[y], :, :], sems.at[r, k])
        for k, (source, to, y) in enumerate(sources)
    ]


def chunk_lanes(r, spot_ref, ring, wide):
    chunk = lax.rem(spot_ref[0] + (LEAP[r] + ring), ring)
    return pl.ds(pl.multiple_of(chunk * wide, wide), wide)


def norm_kernel(slot, examples, *refs):
    spot_ref, lengths_ref = refs[:2]
    pieces = refs[5:15]
    out_ref, ca_ref, cf_ref, pa_ref, pf_ref, sa_ref, sf_ref, acc_ref, sems = refs[15:24]
    x_ref, va_ref, vf_ref, load_sems = refs[24:]
    loads = [
        pltpu.make_async_copy(source, to, load_sems.at[k])
        for k, (source, to) in enumerate(zip(refs[2:5], (x_ref, va_ref, vf_ref)))
    ]
    for load in loads:
        load.start()
    rows_a, width = va_ref.shape
    rows_f = vf_ref.shape[0]
    ring = ca_ref.shape[0]
    wide = width // ring
    steps = x_ref.shape[1] // wide
    per = wide // slot
    copies = [column_copies(r, spot_ref, pieces, ca_ref, cf_ref, sems) for r in range(ring)]
    for group in copies:
        for copy in group:
            copy.start()
    loads[1].wait()
    loads[2].wait()
    pa_ref[...] = 1.0 / (jnp.sqrt(va_ref[...].astype(jnp.float32)) + epsilon)
    pf_ref[...] = 1.0 / (jnp.sqrt(vf_ref[...].astype(jnp.float32)) + epsilon)
    acc_ref[...] = jnp.zeros_like(acc_ref)
    loads[0].wait()
    position = lax.broadcasted_iota(jnp.int32, (x_ref.shape[0], wide), 1)
    for step in range(steps):
        x = x_ref[:, step * wide : (step + 1) * wide]
        for j in range(per):
            live = lengths_ref[step * per + j]
            keep = (position >= j * slot) & (position < j * slot + live)
            chosen = jnp.where(keep, x, jnp.zeros_like(x))
            sa_ref[step, j * rows_a : (j + 1) * rows_a, :] = chosen[:rows_a]
            sf_ref[step, j * rows_f : (j + 1) * rows_f, :] = chosen[rows_a:]
    for r in range(ring):
        for copy in copies[r]:
            copy.wait()
        lanes = chunk_lanes(r, spot_ref, ring, wide)

        @pl.loop(0, steps)
        def _(step):
            span = pl.ds(pl.multiple_of(step * wide, wide), wide)
            sums = [jnp.zeros((8, wide), jnp.float32) for _ in range(per)]
            for s_ref, c_ref, p_ref, rows in (
                (sa_ref, ca_ref, pa_ref, rows_a),
                (sf_ref, cf_ref, pf_ref, rows_f),
            ):
                tile = lax.dot_general(
                    s_ref[step],
                    c_ref[r, :, :, :, span].reshape(wide, wide),
                    (((1,), (1,)), ((), ())),
                    preferred_element_type=jnp.float32,
                )
                precond = p_ref[:, lanes]
                for j in range(per):
                    mine = tile[j * rows : (j + 1) * rows]
                    share = mine * mine * precond
                    sums[j] = sums[j] + jnp.sum(share.reshape(-1, 8, wide), axis=0)
            for j in range(per):
                acc_ref[step * per + j] += sums[j]

    column = jnp.sum(jnp.sum(acc_ref[...], axis=1), axis=1, keepdims=True)
    lane = lax.broadcasted_iota(jnp.int32, (examples, 128), 1)
    own = lax.broadcasted_iota(jnp.int32, (examples, 128), 0)
    row = jnp.sum(jnp.where(lane == own, column, 0.0), axis=0, keepdims=True)
    out_ref[...] = jnp.broadcast_to(row, out_ref.shape)


VMEM_SPEC = pl.BlockSpec(memory_space=pltpu.VMEM)
SMEM_SPEC = pl.BlockSpec(memory_space=pltpu.SMEM)
ANY_SPEC = pl.BlockSpec(memory_space=pl.ANY)
HBM_SPEC = pl.BlockSpec(memory_space=pltpu.HBM)


def column_scratch(pieces):
    ring, run, rows, tokens = pieces[0].shape
    return pltpu.VMEM((ring, run, ring, rows, tokens), pieces[0].dtype)


def norms(spot, lengths, x, va, vf, pieces, peers):
    examples = lengths.shape[0]
    ring = pieces[0].shape[0]
    wide = va.shape[1] // ring
    slot = x.shape[1] // examples
    steps = x.shape[1] // wide
    per = wide // slot
    return pl.pallas_call(
        functools.partial(norm_kernel, slot, examples),
        out_shape=jax.ShapeDtypeStruct((peers, 128), jnp.float32),
        in_specs=[SMEM_SPEC, SMEM_SPEC] + [HBM_SPEC] * 3 + [ANY_SPEC] * 10,
        out_specs=VMEM_SPEC,
        scratch_shapes=[
            column_scratch(pieces),
            column_scratch(pieces),
            pltpu.VMEM(va.shape, jnp.float32),
            pltpu.VMEM(vf.shape, jnp.float32),
            pltpu.VMEM((steps, per * va.shape[0], wide), x.dtype),
            pltpu.VMEM((steps, per * vf.shape[0], wide), x.dtype),
            pltpu.VMEM((examples, 8, wide), jnp.float32),
            pltpu.SemaphoreType.DMA((ring, 2 * ring)),
            pltpu.VMEM(x.shape, x.dtype),
            pltpu.VMEM(va.shape, va.dtype),
            pltpu.VMEM(vf.shape, vf.dtype),
            pltpu.SemaphoreType.DMA((3,)),
        ],
        name="norms",
    )(spot, lengths, x, va, vf, *pieces)


def adam_kernel(slot, examples, *refs):
    spot_ref, parts_ref, lengths_ref, group_row_ref, group_col_ref = refs[:5]
    pieces = refs[12:22]
    outs = refs[22:28]
    ca_ref, cf_ref, sems, x_ref = refs[28:32]
    olds = refs[32:38]
    news = refs[38:44]
    load_sems, store_sems = refs[44:]
    loads = [
        pltpu.make_async_copy(source, to, load_sems.at[k])
        for k, (source, to) in enumerate(zip(refs[5:12], (x_ref, *olds)))
    ]
    for load in loads:
        load.start()
    tokens = x_ref.shape[1]
    rows_a, width = olds[0].shape
    rows = x_ref.shape[0]
    ring = ca_ref.shape[0]
    wide = width // ring
    copies = [column_copies(r, spot_ref, pieces, ca_ref, cf_ref, sems) for r in range(ring)]
    for group in copies:
        for copy in group:
            copy.start()
    norm_row = jnp.sum(parts_ref[...], axis=0, keepdims=True)
    strength = jnp.sqrt(norm_row + norm_epsilon)
    shape = (examples, strength.shape[1])
    lane = lax.broadcasted_iota(jnp.int32, shape, 1)
    own = lax.broadcasted_iota(jnp.int32, shape, 0)
    same = (group_row_ref[...] == group_col_ref[...]) & (lane < examples)
    total = jnp.sum(jnp.where(same, strength, 0.0), axis=1, keepdims=True)
    count = jnp.sum(jnp.where(same, 1.0, 0.0), axis=1, keepdims=True)
    mine = jnp.sum(jnp.where(lane == own, strength, 0.0), axis=1, keepdims=True)
    weight = count * mine / total
    token = lax.broadcasted_iota(jnp.int32, (examples, tokens), 1)
    start = lax.broadcasted_iota(jnp.int32, (examples, tokens), 0) * slot
    live = (token >= start) & (token < start + lengths_ref[...])
    token_weight = jnp.sum(jnp.where(live, weight, 0.0), axis=0, keepdims=True)
    on = jnp.sum(jnp.where(live, 1.0, 0.0), axis=0, keepdims=True)
    for load in loads:
        load.wait()
    x = jnp.where(on > 0.0, x_ref[...].astype(jnp.float32), 0.0)
    scaled = (x * token_weight).astype(jnp.bfloat16)
    stores = []
    for r in range(ring):
        for copy in copies[r]:
            copy.wait()
        lanes = chunk_lanes(r, spot_ref, ring, wide)
        for low, high, c_ref, first in ((0, rows_a, ca_ref, 0), (rows_a, rows, cf_ref, 3)):
            product = lax.dot_general(
                scaled[low:high],
                c_ref[r].reshape(wide, tokens),
                (((1,), (1,)), ((), ())),
                preferred_element_type=jnp.float32,
            )
            gradient = product / examples
            wide_old = olds[first][:, lanes].astype(jnp.float32)
            moment_new = (
                first_decay * olds[first + 1][:, lanes].astype(jnp.float32)
                + (1.0 - first_decay) * gradient
            )
            second_new = (
                second_decay * olds[first + 2][:, lanes].astype(jnp.float32)
                + (1.0 - second_decay) * gradient * gradient
            )
            step_dir = moment_new / first_bias / (jnp.sqrt(second_new / second_bias) + epsilon)
            updated = wide_old - learn_rate * (step_dir + weight_decay * wide_old)
            news[first][:, lanes] = updated.astype(jnp.bfloat16)
            news[first + 1][:, lanes] = moment_new.astype(jnp.bfloat16)
            news[first + 2][:, lanes] = second_new.astype(jnp.bfloat16)
            for k in range(first, first + 3):
                store = pltpu.make_async_copy(
                    news[k].at[:, lanes], outs[k].at[:, lanes], store_sems.at[r, k]
                )
                store.start()
                stores.append(store)
    for store in stores:
        store.wait()


def adam(spot, parts, lengths, groups, x, states, pieces):
    examples = lengths.shape[0]
    ring = pieces[0].shape[0]
    group_row = jnp.pad(groups, (0, parts.shape[1] - examples)).reshape(1, -1)
    return pl.pallas_call(
        functools.partial(adam_kernel, x.shape[1] // examples, examples),
        out_shape=tuple(jax.ShapeDtypeStruct(s.shape, s.dtype) for s in states),
        in_specs=[SMEM_SPEC] + [VMEM_SPEC] * 4 + [HBM_SPEC] * 7 + [ANY_SPEC] * 10,
        out_specs=(ANY_SPEC,) * 6,
        scratch_shapes=[
            column_scratch(pieces),
            column_scratch(pieces),
            pltpu.SemaphoreType.DMA((ring, 2 * ring)),
            pltpu.VMEM(x.shape, x.dtype),
            *[pltpu.VMEM(s.shape, s.dtype) for s in states],
            *[pltpu.VMEM(s.shape, s.dtype) for s in states],
            pltpu.SemaphoreType.DMA((7,)),
            pltpu.SemaphoreType.DMA((ring, 6)),
        ],
        name="adam",
    )(spot, parts, lengths.reshape(-1, 1), group_row, groups.reshape(-1, 1), x, *states, *pieces)


def plane_pieces(value, axis_first, axis_second):
    block = jnp.stack(ring_pieces(value, axis_first))
    behind, ahead = turn(block, axis_second, 1), turn(block, axis_second, -1)
    return block, behind, ahead


def far_pieces(behind, ahead, axis):
    half = behind.shape[0] // 2
    return turn(behind[:half], axis, 1), turn(ahead[half:], axis, -1)


def per_device(
    attention_input,
    feedforward_input,
    attention_cotangent,
    feedforward_cotangent,
    lengths,
    groups,
    attention_weight,
    attention_moment,
    attention_second,
    feedforward_weight,
    feedforward_moment,
    feedforward_second,
):
    run = z_run((attention_cotangent, feedforward_cotangent))
    tokens = attention_cotangent.shape[1]
    near_a = plane_pieces(run[:, :, :tokens], "fsdp_0", "fsdp_2")
    near_f = plane_pieces(run[:, :, tokens:], "fsdp_2", "fsdp_0")
    width = attention_input.shape[1]
    packed = packed_inputs((attention_input, feedforward_input))
    packed = lax.optimization_barrier((packed, near_a[0], near_f[0]))[0]
    met = lax.all_gather(packed, "dp_0", axis=0, tiled=False)
    met = lax.all_gather(met, "dp_1", axis=1, tiled=False)
    rows = attention_input.shape[0] + feedforward_input.shape[0]
    inputs = unpacked_inputs(met.reshape(-1, *packed.shape), rows, width)
    far_a = far_pieces(near_a[1], near_a[2], "fsdp_2")
    far_f = far_pieces(near_f[1], near_f[2], "fsdp_0")
    pieces = near_a + far_a + near_f + far_f
    spot = jnp.stack([lax.axis_index("fsdp_0"), lax.axis_index("fsdp_2")]).astype(jnp.int32)
    peers = lax.axis_size(FSDP)
    spread = norms(spot, lengths, inputs, attention_second, feedforward_second, pieces, peers)
    parts = sum_shares(spread)
    states = (
        attention_weight,
        attention_moment,
        attention_second,
        feedforward_weight,
        feedforward_moment,
        feedforward_second,
    )
    return adam(spot, parts, lengths, groups, inputs, states, pieces)


def solution(mesh):
    finer = Mesh(
        mesh.devices.reshape(4, 2, 4, 8, 4), ("dp_0", "dp_1", "fsdp_0", "fsdp_1", "fsdp_2")
    )
    in_specs = (
        P(FSDP, DP),
        P(FSDP, DP),
        P(DP_FSDP, None),
        P(DP_FSDP, None),
        P(),
        P(),
        P(FSDP, DP),
        P(FSDP, DP),
        P(FSDP, DP),
        P(FSDP, DP),
        P(FSDP, DP),
        P(FSDP, DP),
    )
    out_specs = (P(FSDP, DP), P(FSDP, DP), P(FSDP, DP), P(FSDP, DP), P(FSDP, DP), P(FSDP, DP))
    return jax.shard_map(
        per_device, mesh=finer, in_specs=in_specs, out_specs=out_specs, check_vma=False
    )
```

```python
import functools

import jax
import jax.numpy as jnp
from jax import lax
from jax.experimental import pallas as pl
from jax.experimental.pallas import tpu as pltpu
from jax.sharding import Mesh
from jax.sharding import PartitionSpec as P

DP = ("dp_0", "dp_1")
FSDP = ("fsdp_0", "fsdp_1", "fsdp_2")
DP_FSDP = ("dp_0", "dp_1", "fsdp_0", "fsdp_1", "fsdp_2")


first_decay = 0.9
second_decay = 0.95
first_bias = 1.0 - 0.9**10
second_bias = 1.0 - 0.95**10
learn_rate = 0.01
weight_decay = 0.1
epsilon = 1e-08
norm_epsilon = 1e-06


def spread_rows(value, axis):
    peers = lax.axis_size(axis)
    spread = jnp.broadcast_to(value[None], (peers,) + value.shape)
    return lax.all_to_all(spread, axis, 0, 0, tiled=True)


def column_plane(arrays):
    both = jnp.concatenate(arrays, axis=1)
    run = spread_rows(both, "fsdp_1")
    plane = spread_rows(run, ("fsdp_0", "fsdp_2"))
    across, deep = lax.axis_size("fsdp_0"), lax.axis_size("fsdp_2")
    return run, plane.reshape(across, deep, *run.shape)


def packed_inputs(arrays):
    both = jnp.concatenate(arrays, axis=0)
    rows, width = both.shape
    lanes = 128
    rest = both[:, lanes:]
    parts = lanes // (width - lanes)
    tail = jnp.concatenate(jnp.split(rest, parts, axis=0), axis=1)
    return jnp.concatenate([both[:, :lanes], tail], axis=0)


def unpacked_inputs(blocks, rows, width):
    count, _, lanes = blocks.shape
    body = blocks[:, :rows]
    rest = width - lanes
    tail = jnp.concatenate([blocks[:, rows:, at : at + rest] for at in range(0, lanes, rest)], axis=1)
    whole = jnp.concatenate([body, tail], axis=2)
    return whole.transpose(1, 0, 2).reshape(rows, count * width)


def sum_shares(spread):
    met = lax.all_to_all(spread, FSDP, 0, 0, tiled=True)
    part = jnp.sum(met, axis=0, keepdims=True)
    return lax.all_gather(part, DP, axis=0, tiled=True)


def column_copies(r, plane_ref, c_ref, sems):
    return [
        pltpu.make_async_copy(plane_ref.at[r, y], c_ref.at[r, :, y, :, :], sems.at[r, y])
        for y in range(plane_ref.shape[1])
    ]


def norm_kernel(slot, examples, *refs):
    lengths_ref, plane_ref = refs[0], refs[4]
    out_ref, c_ref, pa_ref, pf_ref, sa_ref, sf_ref, acc_ref, sems = refs[5:13]
    x_ref, va_ref, vf_ref, load_sems = refs[13:]
    loads = [
        pltpu.make_async_copy(source, to, load_sems.at[k])
        for k, (source, to) in enumerate(zip(refs[1:4], (x_ref, va_ref, vf_ref)))
    ]
    for load in loads:
        load.start()
    rows_a, width = va_ref.shape
    rows_f = vf_ref.shape[0]
    ring = c_ref.shape[0]
    wide = width // ring
    steps = x_ref.shape[1] // wide
    per = wide // slot
    copies = [column_copies(r, plane_ref, c_ref, sems) for r in range(ring)]
    for group in copies:
        for copy in group:
            copy.start()
    loads[1].wait()
    loads[2].wait()
    pa_ref[...] = 1.0 / (jnp.sqrt(va_ref[...].astype(jnp.float32)) + epsilon)
    pf_ref[...] = 1.0 / (jnp.sqrt(vf_ref[...].astype(jnp.float32)) + epsilon)
    acc_ref[...] = jnp.zeros_like(acc_ref)
    loads[0].wait()
    position = lax.broadcasted_iota(jnp.int32, (x_ref.shape[0], wide), 1)
    for step in range(steps):
        x = x_ref[:, step * wide : (step + 1) * wide]
        for j in range(per):
            live = lengths_ref[step * per + j]
            keep = (position >= j * slot) & (position < j * slot + live)
            chosen = jnp.where(keep, x, jnp.zeros_like(x))
            sa_ref[step, j * rows_a : (j + 1) * rows_a, :] = chosen[:rows_a]
            sf_ref[step, j * rows_f : (j + 1) * rows_f, :] = chosen[rows_a:]
    for r in range(ring):
        for copy in copies[r]:
            copy.wait()
        lanes = slice(r * wide, (r + 1) * wide)

        for step in range(steps):
            sums = [jnp.zeros((8, wide), jnp.float32) for _ in range(per)]
            for s_ref, p_ref, rows, block in (
                (sa_ref, pa_ref, rows_a, step),
                (sf_ref, pf_ref, rows_f, step + steps),
            ):
                span = pl.ds(pl.multiple_of(block * wide, wide), wide)
                tile = lax.dot_general(
                    s_ref[step],
                    c_ref[r, :, :, :, span].reshape(wide, wide),
                    (((1,), (1,)), ((), ())),
                    preferred_element_type=jnp.float32,
                )
                precond = p_ref[:, lanes]
                for j in range(per):
                    mine = tile[j * rows : (j + 1) * rows]
                    share = mine * mine * precond
                    sums[j] = sums[j] + jnp.sum(share.reshape(-1, 8, wide), axis=0)
            for j in range(per):
                acc_ref[step * per + j] += sums[j]

    column = jnp.sum(jnp.sum(acc_ref[...], axis=1), axis=1, keepdims=True)
    lane = lax.broadcasted_iota(jnp.int32, (examples, 128), 1)
    own = lax.broadcasted_iota(jnp.int32, (examples, 128), 0)
    row = jnp.sum(jnp.where(lane == own, column, 0.0), axis=0, keepdims=True)
    out_ref[...] = jnp.broadcast_to(row, out_ref.shape)


VMEM_SPEC = pl.BlockSpec(memory_space=pltpu.VMEM)
SMEM_SPEC = pl.BlockSpec(memory_space=pltpu.SMEM)
ANY_SPEC = pl.BlockSpec(memory_space=pl.ANY)
HBM_SPEC = pl.BlockSpec(memory_space=pltpu.HBM)


def column_scratch(plane):
    across, deep, run, rows, tokens = plane.shape
    return pltpu.VMEM((across, run, deep, rows, tokens), plane.dtype)


def norms(lengths, x, va, vf, plane, peers):
    examples = lengths.shape[0]
    ring = plane.shape[0]
    wide = va.shape[1] // ring
    slot = x.shape[1] // examples
    steps = x.shape[1] // wide
    per = wide // slot
    return pl.pallas_call(
        functools.partial(norm_kernel, slot, examples),
        out_shape=jax.ShapeDtypeStruct((peers, 128), jnp.float32),
        in_specs=[SMEM_SPEC] + [HBM_SPEC] * 3 + [ANY_SPEC],
        out_specs=VMEM_SPEC,
        scratch_shapes=[
            column_scratch(plane),
            pltpu.VMEM(va.shape, jnp.float32),
            pltpu.VMEM(vf.shape, jnp.float32),
            pltpu.VMEM((steps, per * va.shape[0], wide), x.dtype),
            pltpu.VMEM((steps, per * vf.shape[0], wide), x.dtype),
            pltpu.VMEM((examples, 8, wide), jnp.float32),
            pltpu.SemaphoreType.DMA((ring, plane.shape[1])),
            pltpu.VMEM(x.shape, x.dtype),
            pltpu.VMEM(va.shape, va.dtype),
            pltpu.VMEM(vf.shape, vf.dtype),
            pltpu.SemaphoreType.DMA((3,)),
        ],
        name="norms",
    )(lengths, x, va, vf, plane)


def adam_kernel(slot, examples, *refs):
    parts_ref, lengths_ref, group_row_ref, group_col_ref = refs[:4]
    plane_ref = refs[11]
    outs = refs[12:18]
    c_ref, sems, x_ref = refs[18:21]
    olds = refs[21:27]
    news = refs[27:33]
    load_sems, store_sems = refs[33:]
    loads = [
        pltpu.make_async_copy(source, to, load_sems.at[k])
        for k, (source, to) in enumerate(zip(refs[4:11], (x_ref, *olds)))
    ]
    for load in loads:
        load.start()
    tokens = x_ref.shape[1]
    rows_a, width = olds[0].shape
    rows = x_ref.shape[0]
    ring = c_ref.shape[0]
    wide = width // ring
    copies = [column_copies(r, plane_ref, c_ref, sems) for r in range(ring)]
    for group in copies:
        for copy in group:
            copy.start()
    norm_row = jnp.sum(parts_ref[...], axis=0, keepdims=True)
    strength = jnp.sqrt(norm_row + norm_epsilon)
    shape = (examples, strength.shape[1])
    lane = lax.broadcasted_iota(jnp.int32, shape, 1)
    own = lax.broadcasted_iota(jnp.int32, shape, 0)
    same = (group_row_ref[...] == group_col_ref[...]) & (lane < examples)
    total = jnp.sum(jnp.where(same, strength, 0.0), axis=1, keepdims=True)
    count = jnp.sum(jnp.where(same, 1.0, 0.0), axis=1, keepdims=True)
    mine = jnp.sum(jnp.where(lane == own, strength, 0.0), axis=1, keepdims=True)
    weight = count * mine / total
    token = lax.broadcasted_iota(jnp.int32, (examples, tokens), 1)
    start = lax.broadcasted_iota(jnp.int32, (examples, tokens), 0) * slot
    live = (token >= start) & (token < start + lengths_ref[...])
    token_weight = jnp.sum(jnp.where(live, weight, 0.0), axis=0, keepdims=True)
    on = jnp.sum(jnp.where(live, 1.0, 0.0), axis=0, keepdims=True)
    for load in loads:
        load.wait()
    x = jnp.where(on > 0.0, x_ref[...].astype(jnp.float32), 0.0)
    scaled = (x * token_weight).astype(jnp.bfloat16)
    stores = []
    for r in range(ring):
        for copy in copies[r]:
            copy.wait()
        lanes = slice(r * wide, (r + 1) * wide)
        for low, high, at, first in ((0, rows_a, 0, 0), (rows_a, rows, tokens, 3)):
            product = lax.dot_general(
                scaled[low:high],
                c_ref[r, :, :, :, at : at + tokens].reshape(wide, tokens),
                (((1,), (1,)), ((), ())),
                preferred_element_type=jnp.float32,
            )
            gradient = product / examples
            wide_old = olds[first][:, lanes].astype(jnp.float32)
            moment_new = (
                first_decay * olds[first + 1][:, lanes].astype(jnp.float32)
                + (1.0 - first_decay) * gradient
            )
            second_new = (
                second_decay * olds[first + 2][:, lanes].astype(jnp.float32)
                + (1.0 - second_decay) * gradient * gradient
            )
            step_dir = moment_new / first_bias / (jnp.sqrt(second_new / second_bias) + epsilon)
            updated = wide_old - learn_rate * (step_dir + weight_decay * wide_old)
            news[first][:, lanes] = updated.astype(jnp.bfloat16)
            news[first + 1][:, lanes] = moment_new.astype(jnp.bfloat16)
            news[first + 2][:, lanes] = second_new.astype(jnp.bfloat16)
            for k in range(first, first + 3):
                store = pltpu.make_async_copy(
                    news[k].at[:, lanes], outs[k].at[:, lanes], store_sems.at[r, k]
                )
                store.start()
                stores.append(store)
    for store in stores:
        store.wait()


def adam(parts, lengths, groups, x, states, plane):
    examples = lengths.shape[0]
    ring = plane.shape[0]
    group_row = jnp.pad(groups, (0, parts.shape[1] - examples)).reshape(1, -1)
    return pl.pallas_call(
        functools.partial(adam_kernel, x.shape[1] // examples, examples),
        out_shape=tuple(jax.ShapeDtypeStruct(s.shape, s.dtype) for s in states),
        in_specs=[VMEM_SPEC] * 4 + [HBM_SPEC] * 7 + [ANY_SPEC],
        out_specs=(ANY_SPEC,) * 6,
        scratch_shapes=[
            column_scratch(plane),
            pltpu.SemaphoreType.DMA((ring, plane.shape[1])),
            pltpu.VMEM(x.shape, x.dtype),
            *[pltpu.VMEM(s.shape, s.dtype) for s in states],
            *[pltpu.VMEM(s.shape, s.dtype) for s in states],
            pltpu.SemaphoreType.DMA((7,)),
            pltpu.SemaphoreType.DMA((ring, 6)),
        ],
        name="adam",
    )(parts, lengths.reshape(-1, 1), group_row, groups.reshape(-1, 1), x, *states, plane)


def per_device(
    attention_input,
    feedforward_input,
    attention_cotangent,
    feedforward_cotangent,
    lengths,
    groups,
    attention_weight,
    attention_moment,
    attention_second,
    feedforward_weight,
    feedforward_moment,
    feedforward_second,
):
    run, plane = column_plane((attention_cotangent, feedforward_cotangent))
    width = attention_input.shape[1]
    packed = packed_inputs((attention_input, feedforward_input))
    packed = lax.optimization_barrier((packed, run))[0]
    met = lax.all_gather(packed, "dp_0", axis=0, tiled=False)
    met = lax.all_gather(met, "dp_1", axis=1, tiled=False)
    rows = attention_input.shape[0] + feedforward_input.shape[0]
    inputs = unpacked_inputs(met.reshape(-1, *packed.shape), rows, width)
    peers = lax.axis_size(FSDP)
    spread = norms(lengths, inputs, attention_second, feedforward_second, plane, peers)
    parts = sum_shares(spread)
    states = (
        attention_weight,
        attention_moment,
        attention_second,
        feedforward_weight,
        feedforward_moment,
        feedforward_second,
    )
    return adam(parts, lengths, groups, inputs, states, plane)


def solution(mesh):
    finer = Mesh(
        mesh.devices.reshape(4, 2, 4, 8, 4), ("dp_0", "dp_1", "fsdp_0", "fsdp_1", "fsdp_2")
    )
    in_specs = (
        P(FSDP, DP),
        P(FSDP, DP),
        P(DP_FSDP, None),
        P(DP_FSDP, None),
        P(),
        P(),
        P(FSDP, DP),
        P(FSDP, DP),
        P(FSDP, DP),
        P(FSDP, DP),
        P(FSDP, DP),
        P(FSDP, DP),
    )
    out_specs = (P(FSDP, DP), P(FSDP, DP), P(FSDP, DP), P(FSDP, DP), P(FSDP, DP), P(FSDP, DP))
    return jax.shard_map(
        per_device, mesh=finer, in_specs=in_specs, out_specs=out_specs, check_vma=False
    )
```

```python
import functools

import jax
import jax.numpy as jnp
from jax import lax
from jax.experimental import pallas as pl
from jax.experimental.pallas import tpu as pltpu
from jax.sharding import Mesh
from jax.sharding import PartitionSpec as P

DP = ("dp_0", "dp_1")
FSDP = ("fsdp_0", "fsdp_1", "fsdp_2")
DP_FSDP = ("dp_0", "dp_1", "fsdp_0", "fsdp_1", "fsdp_2")


first_decay = 0.9
second_decay = 0.95
first_bias = 1.0 - 0.9**10
second_bias = 1.0 - 0.95**10
learn_rate = 0.01
weight_decay = 0.1
epsilon = 1e-08
norm_epsilon = 1e-06


LEAP = (0, -1, 1, 2)


def turn(value, axis, by):
    size = lax.axis_size(axis)
    return lax.ppermute(value, axis, [(i, (i + by) % size) for i in range(size)])


def ring_pieces(value, axis):
    return [value] + [turn(value, axis, -leap) for leap in LEAP[1:]]


def z_run(arrays):
    both = jnp.concatenate(arrays, axis=1)
    peers = lax.axis_size("fsdp_1")
    spread = jnp.broadcast_to(both[None], (peers,) + both.shape)
    return lax.all_to_all(spread, "fsdp_1", 0, 0, tiled=False)


def packed_inputs(arrays):
    both = jnp.concatenate(arrays, axis=0)
    rows, width = both.shape
    lanes = 128
    rest = both[:, lanes:]
    parts = lanes // (width - lanes)
    tail = jnp.concatenate(jnp.split(rest, parts, axis=0), axis=1)
    return jnp.concatenate([both[:, :lanes], tail], axis=0)


def unpacked_inputs(blocks, rows, width):
    count, _, lanes = blocks.shape
    body = blocks[:, :rows]
    rest = width - lanes
    tail = jnp.concatenate([blocks[:, rows:, at : at + rest] for at in range(0, lanes, rest)], axis=1)
    whole = jnp.concatenate([body, tail], axis=2)
    return whole.transpose(1, 0, 2).reshape(rows, count * width)


def sum_shares(spread):
    met = lax.all_to_all(spread, FSDP, 0, 0, tiled=True)
    part = jnp.sum(met, axis=0, keepdims=True)
    return lax.all_gather(part, DP, axis=0, tiled=True)


def column_copies(r, spot_ref, pieces, ca_ref, cf_ref, sems):
    ring = ca_ref.shape[2]
    at_y = [lax.rem(spot_ref[1] + (leap + ring), ring) for leap in LEAP]
    sources = [(piece.at[r], ca_ref) for piece in pieces[:ring]]
    sources += [(pieces[ring + r].at[k], cf_ref) for k in range(ring)]
    return [
        pltpu.make_async_copy(source, to.at[r, :, at_y[k % ring], :, :], sems.at[r, k])
        for k, (source, to) in enumerate(sources)
    ]


def chunk_lanes(r, spot_ref, ring, wide):
    chunk = lax.rem(spot_ref[0] + (LEAP[r] + ring), ring)
    return pl.ds(pl.multiple_of(chunk * wide, wide), wide)


def norm_kernel(slot, examples, *refs):
    spot_ref, lengths_ref = refs[:2]
    pieces = refs[5:13]
    out_ref, ca_ref, cf_ref, pa_ref, pf_ref, sa_ref, sf_ref, acc_ref, sems = refs[13:22]
    x_ref, va_ref, vf_ref, load_sems = refs[22:]
    loads = [
        pltpu.make_async_copy(source, to, load_sems.at[k])
        for k, (source, to) in enumerate(zip(refs[2:5], (x_ref, va_ref, vf_ref)))
    ]
    for load in loads:
        load.start()
    rows_a, width = va_ref.shape
    rows_f = vf_ref.shape[0]
    ring = ca_ref.shape[0]
    wide = width // ring
    steps = x_ref.shape[1] // wide
    per = wide // slot
    copies = [column_copies(r, spot_ref, pieces, ca_ref, cf_ref, sems) for r in range(ring)]
    for group in copies:
        for copy in group:
            copy.start()
    loads[1].wait()
    loads[2].wait()
    pa_ref[...] = 1.0 / (jnp.sqrt(va_ref[...].astype(jnp.float32)) + epsilon)
    pf_ref[...] = 1.0 / (jnp.sqrt(vf_ref[...].astype(jnp.float32)) + epsilon)
    acc_ref[...] = jnp.zeros_like(acc_ref)
    loads[0].wait()
    position = lax.broadcasted_iota(jnp.int32, (x_ref.shape[0], wide), 1)
    for step in range(steps):
        x = x_ref[:, step * wide : (step + 1) * wide]
        for j in range(per):
            live = lengths_ref[step * per + j]
            keep = (position >= j * slot) & (position < j * slot + live)
            chosen = jnp.where(keep, x, jnp.zeros_like(x))
            sa_ref[step, j * rows_a : (j + 1) * rows_a, :] = chosen[:rows_a]
            sf_ref[step, j * rows_f : (j + 1) * rows_f, :] = chosen[rows_a:]
    for r in range(ring):
        for copy in copies[r]:
            copy.wait()
        lanes = chunk_lanes(r, spot_ref, ring, wide)

        for step in range(steps):
            span = slice(step * wide, (step + 1) * wide)
            sums = [jnp.zeros((8, wide), jnp.float32) for _ in range(per)]
            for s_ref, c_ref, p_ref, rows in (
                (sa_ref, ca_ref, pa_ref, rows_a),
                (sf_ref, cf_ref, pf_ref, rows_f),
            ):
                tile = lax.dot_general(
                    s_ref[step],
                    c_ref[r, :, :, :, span].reshape(wide, wide),
                    (((1,), (1,)), ((), ())),
                    preferred_element_type=jnp.float32,
                )
                precond = p_ref[:, lanes]
                for j in range(per):
                    mine = tile[j * rows : (j + 1) * rows]
                    share = mine * mine * precond
                    sums[j] = sums[j] + jnp.sum(share.reshape(-1, 8, wide), axis=0)
            for j in range(per):
                acc_ref[step * per + j] += sums[j]

    column = jnp.sum(jnp.sum(acc_ref[...], axis=1), axis=1, keepdims=True)
    lane = lax.broadcasted_iota(jnp.int32, (examples, 128), 1)
    own = lax.broadcasted_iota(jnp.int32, (examples, 128), 0)
    row = jnp.sum(jnp.where(lane == own, column, 0.0), axis=0, keepdims=True)
    out_ref[...] = jnp.broadcast_to(row, out_ref.shape)


VMEM_SPEC = pl.BlockSpec(memory_space=pltpu.VMEM)
SMEM_SPEC = pl.BlockSpec(memory_space=pltpu.SMEM)
ANY_SPEC = pl.BlockSpec(memory_space=pl.ANY)
HBM_SPEC = pl.BlockSpec(memory_space=pltpu.HBM)


def column_scratch(pieces):
    ring, run, rows, tokens = pieces[0].shape
    return pltpu.VMEM((ring, run, ring, rows, tokens), pieces[0].dtype)


def norms(spot, lengths, x, va, vf, pieces, peers):
    examples = lengths.shape[0]
    ring = pieces[0].shape[0]
    wide = va.shape[1] // ring
    slot = x.shape[1] // examples
    steps = x.shape[1] // wide
    per = wide // slot
    return pl.pallas_call(
        functools.partial(norm_kernel, slot, examples),
        out_shape=jax.ShapeDtypeStruct((peers, 128), jnp.float32),
        in_specs=[SMEM_SPEC, SMEM_SPEC] + [HBM_SPEC] * 3 + [ANY_SPEC] * 8,
        out_specs=VMEM_SPEC,
        scratch_shapes=[
            column_scratch(pieces),
            column_scratch(pieces),
            pltpu.VMEM(va.shape, jnp.float32),
            pltpu.VMEM(vf.shape, jnp.float32),
            pltpu.VMEM((steps, per * va.shape[0], wide), x.dtype),
            pltpu.VMEM((steps, per * vf.shape[0], wide), x.dtype),
            pltpu.VMEM((examples, 8, wide), jnp.float32),
            pltpu.SemaphoreType.DMA((ring, 2 * ring)),
            pltpu.VMEM(x.shape, x.dtype),
            pltpu.VMEM(va.shape, va.dtype),
            pltpu.VMEM(vf.shape, vf.dtype),
            pltpu.SemaphoreType.DMA((3,)),
        ],
        name="norms",
    )(spot, lengths, x, va, vf, *pieces)


def adam_kernel(slot, examples, *refs):
    spot_ref, parts_ref, lengths_ref, group_row_ref, group_col_ref = refs[:5]
    pieces = refs[12:20]
    outs = refs[20:26]
    ca_ref, cf_ref, sems, x_ref = refs[26:30]
    olds = refs[30:36]
    news = refs[36:42]
    load_sems, store_sems = refs[42:]
    loads = [
        pltpu.make_async_copy(source, to, load_sems.at[k])
        for k, (source, to) in enumerate(zip(refs[5:12], (x_ref, *olds)))
    ]
    for load in loads:
        load.start()
    tokens = x_ref.shape[1]
    rows_a, width = olds[0].shape
    rows = x_ref.shape[0]
    ring = ca_ref.shape[0]
    wide = width // ring
    copies = [column_copies(r, spot_ref, pieces, ca_ref, cf_ref, sems) for r in range(ring)]
    for group in copies:
        for copy in group:
            copy.start()
    norm_row = jnp.sum(parts_ref[...], axis=0, keepdims=True)
    strength = jnp.sqrt(norm_row + norm_epsilon)
    shape = (examples, strength.shape[1])
    lane = lax.broadcasted_iota(jnp.int32, shape, 1)
    own = lax.broadcasted_iota(jnp.int32, shape, 0)
    same = (group_row_ref[...] == group_col_ref[...]) & (lane < examples)
    total = jnp.sum(jnp.where(same, strength, 0.0), axis=1, keepdims=True)
    count = jnp.sum(jnp.where(same, 1.0, 0.0), axis=1, keepdims=True)
    mine = jnp.sum(jnp.where(lane == own, strength, 0.0), axis=1, keepdims=True)
    weight = count * mine / total
    token = lax.broadcasted_iota(jnp.int32, (examples, tokens), 1)
    start = lax.broadcasted_iota(jnp.int32, (examples, tokens), 0) * slot
    live = (token >= start) & (token < start + lengths_ref[...])
    token_weight = jnp.sum(jnp.where(live, weight, 0.0), axis=0, keepdims=True)
    on = jnp.sum(jnp.where(live, 1.0, 0.0), axis=0, keepdims=True)
    for load in loads:
        load.wait()
    x = jnp.where(on > 0.0, x_ref[...].astype(jnp.float32), 0.0)
    scaled = (x * token_weight).astype(jnp.bfloat16)
    stores = []
    for r in range(ring):
        for copy in copies[r]:
            copy.wait()
        lanes = chunk_lanes(r, spot_ref, ring, wide)
        for low, high, c_ref, first in ((0, rows_a, ca_ref, 0), (rows_a, rows, cf_ref, 3)):
            product = lax.dot_general(
                scaled[low:high],
                c_ref[r].reshape(wide, tokens),
                (((1,), (1,)), ((), ())),
                preferred_element_type=jnp.float32,
            )
            gradient = product / examples
            wide_old = olds[first][:, lanes].astype(jnp.float32)
            moment_new = (
                first_decay * olds[first + 1][:, lanes].astype(jnp.float32)
                + (1.0 - first_decay) * gradient
            )
            second_new = (
                second_decay * olds[first + 2][:, lanes].astype(jnp.float32)
                + (1.0 - second_decay) * gradient * gradient
            )
            step_dir = moment_new / first_bias / (jnp.sqrt(second_new / second_bias) + epsilon)
            updated = wide_old - learn_rate * (step_dir + weight_decay * wide_old)
            news[first][:, lanes] = updated.astype(jnp.bfloat16)
            news[first + 1][:, lanes] = moment_new.astype(jnp.bfloat16)
            news[first + 2][:, lanes] = second_new.astype(jnp.bfloat16)
            for k in range(first, first + 3):
                store = pltpu.make_async_copy(
                    news[k].at[:, lanes], outs[k].at[:, lanes], store_sems.at[r, k]
                )
                store.start()
                stores.append(store)
    for store in stores:
        store.wait()


def adam(spot, parts, lengths, groups, x, states, pieces):
    examples = lengths.shape[0]
    ring = pieces[0].shape[0]
    group_row = jnp.pad(groups, (0, parts.shape[1] - examples)).reshape(1, -1)
    return pl.pallas_call(
        functools.partial(adam_kernel, x.shape[1] // examples, examples),
        out_shape=tuple(jax.ShapeDtypeStruct(s.shape, s.dtype) for s in states),
        in_specs=[SMEM_SPEC] + [VMEM_SPEC] * 4 + [HBM_SPEC] * 7 + [ANY_SPEC] * 8,
        out_specs=(ANY_SPEC,) * 6,
        scratch_shapes=[
            column_scratch(pieces),
            column_scratch(pieces),
            pltpu.SemaphoreType.DMA((ring, 2 * ring)),
            pltpu.VMEM(x.shape, x.dtype),
            *[pltpu.VMEM(s.shape, s.dtype) for s in states],
            *[pltpu.VMEM(s.shape, s.dtype) for s in states],
            pltpu.SemaphoreType.DMA((7,)),
            pltpu.SemaphoreType.DMA((ring, 6)),
        ],
        name="adam",
    )(spot, parts, lengths.reshape(-1, 1), group_row, groups.reshape(-1, 1), x, *states, *pieces)


def plane_pieces(value, axis_first, axis_second):
    block = jnp.stack(ring_pieces(value, axis_first))
    return tuple(ring_pieces(block, axis_second))


def per_device(
    attention_input,
    feedforward_input,
    attention_cotangent,
    feedforward_cotangent,
    lengths,
    groups,
    attention_weight,
    attention_moment,
    attention_second,
    feedforward_weight,
    feedforward_moment,
    feedforward_second,
):
    run = z_run((attention_cotangent, feedforward_cotangent))
    tokens = attention_cotangent.shape[1]
    near_a = plane_pieces(run[:, :, :tokens], "fsdp_0", "fsdp_2")
    near_f = plane_pieces(run[:, :, tokens:], "fsdp_2", "fsdp_0")
    width = attention_input.shape[1]
    packed = packed_inputs((attention_input, feedforward_input))
    packed = lax.optimization_barrier((packed, near_a[0], near_f[0]))[0]
    met = lax.all_gather(packed, "dp_0", axis=0, tiled=False)
    met = lax.all_gather(met, "dp_1", axis=1, tiled=False)
    rows = attention_input.shape[0] + feedforward_input.shape[0]
    inputs = unpacked_inputs(met.reshape(-1, *packed.shape), rows, width)
    pieces = near_a + near_f
    spot = jnp.stack([lax.axis_index("fsdp_0"), lax.axis_index("fsdp_2")]).astype(jnp.int32)
    peers = lax.axis_size(FSDP)
    spread = norms(spot, lengths, inputs, attention_second, feedforward_second, pieces, peers)
    parts = sum_shares(spread)
    states = (
        attention_weight,
        attention_moment,
        attention_second,
        feedforward_weight,
        feedforward_moment,
        feedforward_second,
    )
    return adam(spot, parts, lengths, groups, inputs, states, pieces)


def solution(mesh):
    finer = Mesh(
        mesh.devices.reshape(4, 2, 4, 8, 4), ("dp_0", "dp_1", "fsdp_0", "fsdp_1", "fsdp_2")
    )
    in_specs = (
        P(FSDP, DP),
        P(FSDP, DP),
        P(DP_FSDP, None),
        P(DP_FSDP, None),
        P(),
        P(),
        P(FSDP, DP),
        P(FSDP, DP),
        P(FSDP, DP),
        P(FSDP, DP),
        P(FSDP, DP),
        P(FSDP, DP),
    )
    out_specs = (P(FSDP, DP), P(FSDP, DP), P(FSDP, DP), P(FSDP, DP), P(FSDP, DP), P(FSDP, DP))
    return jax.shard_map(
        per_device, mesh=finer, in_specs=in_specs, out_specs=out_specs, check_vma=False
    )
```

```python
import functools

import jax
import jax.numpy as jnp
from jax import lax
from jax.experimental import pallas as pl
from jax.experimental.pallas import tpu as pltpu
from jax.sharding import Mesh
from jax.sharding import PartitionSpec as P

DP = ("dp_0", "dp_1")
FSDP = ("fsdp_0", "fsdp_1", "fsdp_2")
DP_FSDP = ("dp_0", "dp_1", "fsdp_0", "fsdp_1", "fsdp_2")


first_decay = 0.9
second_decay = 0.95
first_bias = 1.0 - 0.9**10
second_bias = 1.0 - 0.95**10
learn_rate = 0.01
weight_decay = 0.1
epsilon = 1e-08
norm_epsilon = 1e-06


LEAP = (0, -1, 1, 2)


def turn(value, axis, by):
    size = lax.axis_size(axis)
    return lax.ppermute(value, axis, [(i, (i + by) % size) for i in range(size)])


def ring_pieces(value, axis):
    return [value] + [turn(value, axis, -leap) for leap in LEAP[1:]]


def spread_rows(value, axis):
    peers = lax.axis_size(axis)
    spread = jnp.broadcast_to(value[None], (peers,) + value.shape)
    return lax.all_to_all(spread, axis, 0, 0, tiled=True)


def z_run(arrays):
    return spread_rows(jnp.concatenate(arrays, axis=1), "fsdp_1")


def packed_inputs(arrays):
    both = jnp.concatenate(arrays, axis=0)
    rows, width = both.shape
    lanes = 128
    rest = both[:, lanes:]
    parts = lanes // (width - lanes)
    tail = jnp.concatenate(jnp.split(rest, parts, axis=0), axis=1)
    return jnp.concatenate([both[:, :lanes], tail], axis=0)


def unpacked_inputs(blocks, rows, width):
    count, _, lanes = blocks.shape
    body = blocks[:, :rows]
    rest = width - lanes
    tail = jnp.concatenate([blocks[:, rows:, at : at + rest] for at in range(0, lanes, rest)], axis=1)
    whole = jnp.concatenate([body, tail], axis=2)
    return whole.transpose(1, 0, 2).reshape(rows, count * width)


def sum_shares(spread):
    met = lax.all_to_all(spread, FSDP, 0, 0, tiled=True)
    part = jnp.sum(met, axis=0, keepdims=True)
    return lax.all_gather(part, DP, axis=0, tiled=True)


def column_copies(r, spot_ref, pieces, ca_ref, cf_ref, sems):
    ring = ca_ref.shape[2]
    at_y = [lax.rem(spot_ref[1] + (leap + ring), ring) for leap in LEAP]
    sources = [(piece.at[r], ca_ref) for piece in pieces[:ring]]
    sources += [(pieces[ring + r].at[k], cf_ref) for k in range(ring)]
    return [
        pltpu.make_async_copy(source, to.at[r, :, at_y[k % ring], :, :], sems.at[r, k])
        for k, (source, to) in enumerate(sources)
    ]


def chunk_lanes(r, spot_ref, ring, wide):
    chunk = lax.rem(spot_ref[0] + (LEAP[r] + ring), ring)
    return pl.ds(pl.multiple_of(chunk * wide, wide), wide)


def norm_kernel(slot, examples, *refs):
    spot_ref, lengths_ref = refs[:2]
    pieces = refs[5:13]
    out_ref, ca_ref, cf_ref, pa_ref, pf_ref, sa_ref, sf_ref, acc_ref, sems = refs[13:22]
    x_ref, va_ref, vf_ref, load_sems = refs[22:]
    loads = [
        pltpu.make_async_copy(source, to, load_sems.at[k])
        for k, (source, to) in enumerate(zip(refs[2:5], (x_ref, va_ref, vf_ref)))
    ]
    for load in loads:
        load.start()
    rows_a, width = va_ref.shape
    rows_f = vf_ref.shape[0]
    ring = ca_ref.shape[0]
    wide = width // ring
    steps = x_ref.shape[1] // wide
    per = wide // slot
    copies = [column_copies(r, spot_ref, pieces, ca_ref, cf_ref, sems) for r in range(ring)]
    for group in copies:
        for copy in group:
            copy.start()
    loads[1].wait()
    loads[2].wait()
    pa_ref[...] = 1.0 / (jnp.sqrt(va_ref[...].astype(jnp.float32)) + epsilon)
    pf_ref[...] = 1.0 / (jnp.sqrt(vf_ref[...].astype(jnp.float32)) + epsilon)
    acc_ref[...] = jnp.zeros_like(acc_ref)
    loads[0].wait()
    position = lax.broadcasted_iota(jnp.int32, (x_ref.shape[0], wide), 1)
    for step in range(steps):
        x = x_ref[:, step * wide : (step + 1) * wide]
        for j in range(per):
            live = lengths_ref[step * per + j]
            keep = (position >= j * slot) & (position < j * slot + live)
            chosen = jnp.where(keep, x, jnp.zeros_like(x))
            sa_ref[step, j * rows_a : (j + 1) * rows_a, :] = chosen[:rows_a]
            sf_ref[step, j * rows_f : (j + 1) * rows_f, :] = chosen[rows_a:]
    for r in range(ring):
        for copy in copies[r]:
            copy.wait()
        lanes = chunk_lanes(r, spot_ref, ring, wide)

        for step in range(steps):
            span = slice(step * wide, (step + 1) * wide)
            sums = [jnp.zeros((8, wide), jnp.float32) for _ in range(per)]
            for s_ref, c_ref, p_ref, rows, at in (
                (sa_ref, ca_ref, pa_ref, rows_a, slice(r * wide, (r + 1) * wide)),
                (sf_ref, cf_ref, pf_ref, rows_f, lanes),
            ):
                tile = lax.dot_general(
                    s_ref[step],
                    c_ref[r, :, :, :, span].reshape(wide, wide),
                    (((1,), (1,)), ((), ())),
                    preferred_element_type=jnp.float32,
                )
                precond = p_ref[:, at]
                for j in range(per):
                    mine = tile[j * rows : (j + 1) * rows]
                    share = mine * mine * precond
                    sums[j] = sums[j] + jnp.sum(share.reshape(-1, 8, wide), axis=0)
            for j in range(per):
                acc_ref[step * per + j] += sums[j]

    column = jnp.sum(jnp.sum(acc_ref[...], axis=1), axis=1, keepdims=True)
    lane = lax.broadcasted_iota(jnp.int32, (examples, 128), 1)
    own = lax.broadcasted_iota(jnp.int32, (examples, 128), 0)
    row = jnp.sum(jnp.where(lane == own, column, 0.0), axis=0, keepdims=True)
    out_ref[...] = jnp.broadcast_to(row, out_ref.shape)


VMEM_SPEC = pl.BlockSpec(memory_space=pltpu.VMEM)
SMEM_SPEC = pl.BlockSpec(memory_space=pltpu.SMEM)
ANY_SPEC = pl.BlockSpec(memory_space=pl.ANY)
HBM_SPEC = pl.BlockSpec(memory_space=pltpu.HBM)


def column_scratch(pieces):
    ring, run, rows, tokens = pieces[0].shape
    return pltpu.VMEM((ring, run, ring, rows, tokens), pieces[0].dtype)


def norms(spot, lengths, x, va, vf, pieces, peers):
    examples = lengths.shape[0]
    ring = pieces[0].shape[0]
    wide = va.shape[1] // ring
    slot = x.shape[1] // examples
    steps = x.shape[1] // wide
    per = wide // slot
    return pl.pallas_call(
        functools.partial(norm_kernel, slot, examples),
        out_shape=jax.ShapeDtypeStruct((peers, 128), jnp.float32),
        in_specs=[SMEM_SPEC, SMEM_SPEC] + [HBM_SPEC] * 3 + [ANY_SPEC] * 8,
        out_specs=VMEM_SPEC,
        scratch_shapes=[
            column_scratch(pieces),
            column_scratch(pieces),
            pltpu.VMEM(va.shape, jnp.float32),
            pltpu.VMEM(vf.shape, jnp.float32),
            pltpu.VMEM((steps, per * va.shape[0], wide), x.dtype),
            pltpu.VMEM((steps, per * vf.shape[0], wide), x.dtype),
            pltpu.VMEM((examples, 8, wide), jnp.float32),
            pltpu.SemaphoreType.DMA((ring, 2 * ring)),
            pltpu.VMEM(x.shape, x.dtype),
            pltpu.VMEM(va.shape, va.dtype),
            pltpu.VMEM(vf.shape, vf.dtype),
            pltpu.SemaphoreType.DMA((3,)),
        ],
        name="norms",
    )(spot, lengths, x, va, vf, *pieces)


def adam_kernel(slot, examples, *refs):
    spot_ref, parts_ref, lengths_ref, group_row_ref, group_col_ref = refs[:5]
    pieces = refs[12:20]
    outs = refs[20:26]
    ca_ref, cf_ref, sems, x_ref = refs[26:30]
    olds = refs[30:36]
    news = refs[36:42]
    load_sems, store_sems = refs[42:]
    loads = [
        pltpu.make_async_copy(source, to, load_sems.at[k])
        for k, (source, to) in enumerate(zip(refs[5:12], (x_ref, *olds)))
    ]
    for load in loads:
        load.start()
    tokens = x_ref.shape[1]
    rows_a, width = olds[0].shape
    rows = x_ref.shape[0]
    ring = ca_ref.shape[0]
    wide = width // ring
    copies = [column_copies(r, spot_ref, pieces, ca_ref, cf_ref, sems) for r in range(ring)]
    for group in copies:
        for copy in group:
            copy.start()
    norm_row = jnp.sum(parts_ref[...], axis=0, keepdims=True)
    strength = jnp.sqrt(norm_row + norm_epsilon)
    shape = (examples, strength.shape[1])
    lane = lax.broadcasted_iota(jnp.int32, shape, 1)
    own = lax.broadcasted_iota(jnp.int32, shape, 0)
    same = (group_row_ref[...] == group_col_ref[...]) & (lane < examples)
    total = jnp.sum(jnp.where(same, strength, 0.0), axis=1, keepdims=True)
    count = jnp.sum(jnp.where(same, 1.0, 0.0), axis=1, keepdims=True)
    mine = jnp.sum(jnp.where(lane == own, strength, 0.0), axis=1, keepdims=True)
    weight = count * mine / total
    token = lax.broadcasted_iota(jnp.int32, (examples, tokens), 1)
    start = lax.broadcasted_iota(jnp.int32, (examples, tokens), 0) * slot
    live = (token >= start) & (token < start + lengths_ref[...])
    token_weight = jnp.sum(jnp.where(live, weight, 0.0), axis=0, keepdims=True)
    on = jnp.sum(jnp.where(live, 1.0, 0.0), axis=0, keepdims=True)
    for load in loads:
        load.wait()
    x = jnp.where(on > 0.0, x_ref[...].astype(jnp.float32), 0.0)
    scaled = (x * token_weight).astype(jnp.bfloat16)
    stores = []
    for r in range(ring):
        for copy in copies[r]:
            copy.wait()
        lanes = chunk_lanes(r, spot_ref, ring, wide)
        own = pl.ds(r * wide, wide)
        for low, high, c_ref, first, at in (
            (0, rows_a, ca_ref, 0, own),
            (rows_a, rows, cf_ref, 3, lanes),
        ):
            product = lax.dot_general(
                scaled[low:high],
                c_ref[r].reshape(wide, tokens),
                (((1,), (1,)), ((), ())),
                preferred_element_type=jnp.float32,
            )
            gradient = product / examples
            wide_old = olds[first][:, at].astype(jnp.float32)
            moment_new = (
                first_decay * olds[first + 1][:, at].astype(jnp.float32)
                + (1.0 - first_decay) * gradient
            )
            second_new = (
                second_decay * olds[first + 2][:, at].astype(jnp.float32)
                + (1.0 - second_decay) * gradient * gradient
            )
            step_dir = moment_new / first_bias / (jnp.sqrt(second_new / second_bias) + epsilon)
            updated = wide_old - learn_rate * (step_dir + weight_decay * wide_old)
            news[first][:, at] = updated.astype(jnp.bfloat16)
            news[first + 1][:, at] = moment_new.astype(jnp.bfloat16)
            news[first + 2][:, at] = second_new.astype(jnp.bfloat16)
            for k in range(first, first + 3):
                store = pltpu.make_async_copy(
                    news[k].at[:, at], outs[k].at[:, at], store_sems.at[r, k]
                )
                store.start()
                stores.append(store)
    for store in stores:
        store.wait()


def adam(spot, parts, lengths, groups, x, states, pieces):
    examples = lengths.shape[0]
    ring = pieces[0].shape[0]
    group_row = jnp.pad(groups, (0, parts.shape[1] - examples)).reshape(1, -1)
    return pl.pallas_call(
        functools.partial(adam_kernel, x.shape[1] // examples, examples),
        out_shape=tuple(jax.ShapeDtypeStruct(s.shape, s.dtype) for s in states),
        in_specs=[SMEM_SPEC] + [VMEM_SPEC] * 4 + [HBM_SPEC] * 7 + [ANY_SPEC] * 8,
        out_specs=(ANY_SPEC,) * 6,
        scratch_shapes=[
            column_scratch(pieces),
            column_scratch(pieces),
            pltpu.SemaphoreType.DMA((ring, 2 * ring)),
            pltpu.VMEM(x.shape, x.dtype),
            *[pltpu.VMEM(s.shape, s.dtype) for s in states],
            *[pltpu.VMEM(s.shape, s.dtype) for s in states],
            pltpu.SemaphoreType.DMA((7,)),
            pltpu.SemaphoreType.DMA((ring, 6)),
        ],
        name="adam",
    )(spot, parts, lengths.reshape(-1, 1), group_row, groups.reshape(-1, 1), x, *states, *pieces)


def per_device(
    attention_input,
    feedforward_input,
    attention_cotangent,
    feedforward_cotangent,
    lengths,
    groups,
    attention_weight,
    attention_moment,
    attention_second,
    feedforward_weight,
    feedforward_moment,
    feedforward_second,
):
    run = z_run((attention_cotangent, feedforward_cotangent))
    tokens = attention_cotangent.shape[1]
    block_a = spread_rows(run[:, :, :tokens], "fsdp_0")
    block_f = jnp.stack(ring_pieces(run[:, :, tokens:], "fsdp_2"))
    near_a = tuple(ring_pieces(block_a, "fsdp_2"))
    near_f = tuple(ring_pieces(block_f, "fsdp_0"))
    width = attention_input.shape[1]
    packed = packed_inputs((attention_input, feedforward_input))
    packed = lax.optimization_barrier((packed, near_a[0], near_f[0]))[0]
    met = lax.all_gather(packed, "dp_0", axis=0, tiled=False)
    met = lax.all_gather(met, "dp_1", axis=1, tiled=False)
    rows = attention_input.shape[0] + feedforward_input.shape[0]
    inputs = unpacked_inputs(met.reshape(-1, *packed.shape), rows, width)
    pieces = near_a + near_f
    spot = jnp.stack([lax.axis_index("fsdp_0"), lax.axis_index("fsdp_2")]).astype(jnp.int32)
    peers = lax.axis_size(FSDP)
    spread = norms(spot, lengths, inputs, attention_second, feedforward_second, pieces, peers)
    parts = sum_shares(spread)
    states = (
        attention_weight,
        attention_moment,
        attention_second,
        feedforward_weight,
        feedforward_moment,
        feedforward_second,
    )
    return adam(spot, parts, lengths, groups, inputs, states, pieces)


def solution(mesh):
    finer = Mesh(
        mesh.devices.reshape(4, 2, 4, 8, 4), ("dp_0", "dp_1", "fsdp_0", "fsdp_1", "fsdp_2")
    )
    in_specs = (
        P(FSDP, DP),
        P(FSDP, DP),
        P(DP_FSDP, None),
        P(DP_FSDP, None),
        P(),
        P(),
        P(FSDP, DP),
        P(FSDP, DP),
        P(FSDP, DP),
        P(FSDP, DP),
        P(FSDP, DP),
        P(FSDP, DP),
    )
    out_specs = (P(FSDP, DP), P(FSDP, DP), P(FSDP, DP), P(FSDP, DP), P(FSDP, DP), P(FSDP, DP))
    return jax.shard_map(
        per_device, mesh=finer, in_specs=in_specs, out_specs=out_specs, check_vma=False
    )
```
